32 devices in a mesh: parts: 2 (over y), fsdp: 8 (over z, x), rep: 2 (over core).
Axes of the slice: x: 2, y: 2, z: 4, core: 2. Of those that a mesh axis runs over, the one named last changes fastest.
Arguments:
- tokens: bfloat16 [2, 4096, 5120], P('rep', ('parts', 'fsdp')), parts along dimension 1, may hold values from -6 to 6
- cotangent: bfloat16 [2, 4096, 8], P('rep', ('parts', 'fsdp')), parts along dimension 1, may hold values from -0.1875 to 0.1875
- params: float32 [16, 5120], P(('parts', 'fsdp')), parts along dimension 0, may hold values from -0.078125 to 0.078125
- momentum: float32 [2, 16, 5120], P('rep', ('parts', 'fsdp')), parts along dimension 1, may hold values from -6 to 6
- indices: int32 [2, 16, 40, 16], P('rep', ('parts', 'fsdp')), parts along dimension 1, may hold values from 0 to 127, all different within a row
Outputs:
- new_params: float32 [16, 5120], P(('parts', 'fsdp')), parts along dimension 0
- new_momentum: float32 [2, 16, 5120], P('rep', ('parts', 'fsdp')), parts along dimension 1
The draws below stay inside these ranges and needn't reach their ends.
There are 2 independent parts, one for each index of `parts`. The reference program is written for one: setup_inputs(seed, part) draws one part's arguments, and reference() takes and returns one part's arrays. A program takes and returns all parts, laid end to end along the dimension named above; each array names one. Nothing has to cross between parts.
Inputs may be any that keep to these rules, and one draw needn't show every extreme that they name: Within each block the 16 indices are distinct.
All inputs are finite; a program needn't handle non-finite values.
Results may differ from the reference program's by a relative error of at most 0.0003.
Values sent between devices are 32-bit elements; how exact they have to be, the bound alone decides.
No kernel may reach another device: no remote copies, remote signals or barrier semaphores. Data moves between devices by JAX's collectives and lax.ppermute only.
A program may use at most 64 MiB of HBM per device.

```python
import jax
import jax.numpy as jnp
from jax import lax

D = 5120
SPAN = 128
TOPK = 16
ROWS = 8
TOKENS = 2048
NCH = 40
N_REP = 2


def with_spikes(array, stream_key, source, target, blocks, factor):
    owner, partner = [(jnp.arange(array.shape[dim]) // (array.shape[dim] // blocks)).reshape([-1 if axis == dim else 1 for axis in range(array.ndim)]) for dim in (source, target)]
    chosen = jax.random.permutation(stream_key, blocks)[partner]
    strong = (owner == chosen) | (owner == (partner + blocks // 2) % blocks)
    return jnp.where(strong, factor * array, array)


def level_of(stream_key, shape, split, least, high):
    loudness, own = 1.0, jax.random.fold_in(stream_key, 6)
    for dim, shards_of in split:
        steps = jnp.exp(jax.random.uniform(jax.random.fold_in(own, dim), (shards_of,), jnp.float32, least / len(split), high / len(split)))
        loudness = loudness * jnp.repeat(steps, shape[dim] // shards_of).reshape([-1 if axis == dim else 1 for axis in range(len(shape))])
    return loudness


def different_ones(own_key, rows, number_of, top, lift):
    sequence = jax.random.permutation(jax.random.fold_in(own_key, 1), number_of)
    boost = sequence
    for power in range(3):
        boost = boost * boost // number_of
    boost = boost * lift // number_of
    tickets = jax.random.randint(jax.random.fold_in(own_key, 2), (rows, number_of), 0, 4096) + boost
    sure = jax.random.permutation(jax.random.fold_in(own_key, 3), rows)[jnp.arange(number_of) % rows]
    tickets = jnp.where(jnp.arange(rows)[:, None] == sure[None, :], 1 << 14, tickets)
    merit = tickets * number_of + jnp.arange(number_of)
    return lax.top_k(merit.astype(jnp.int32), top)[1].astype(jnp.int32)


def centred(own_key, shape, spread, reach, cuts=(), kind=jnp.bfloat16):
    array = spread * jax.random.normal(own_key, shape, jnp.float32)
    if cuts:
        array = array * level_of(own_key, shape, cuts, -0.22, 0.18)
    return jnp.clip(array, -reach, reach).astype(kind)


def noise_with(rng, extent, spread, bound, cuts, heavy, kind=jnp.bfloat16):
    values = spread * jax.random.normal(rng, extent, jnp.float32)
    if cuts:
        values = values * level_of(rng, extent, cuts, -0.22, 0.18)
    return jnp.clip(with_spikes(values, jax.random.fold_in(rng, 3), *heavy), -bound, bound).astype(kind)


def setup_inputs(seed: int = 0, part: int = 0) -> dict:
    key_of = jax.random.split(jax.random.key(seed), 6)
    part_splits = jax.random.split(jax.random.fold_in(key_of[5], part), 6)
    return {
        "tokens": centred(part_splits[0], (N_REP, TOKENS, D), 1.0, 6.0, ((0, 2), (1, 8))),
        "cotangent": noise_with(part_splits[1], (N_REP, TOKENS, ROWS), (TOKENS ** -0.5), 0.1875, ((0, 2), (1, 8)), (1, 2, 8, 2.0)),
        "params": centred(part_splits[2], (ROWS, D), D ** -0.5, 0.078125, ((0, 8),), jnp.float32),
        "momentum": centred(part_splits[3], (N_REP, ROWS, D), 1.0, 6.0, ((0, 2), (1, 8)), jnp.float32),
        "indices": different_ones(part_splits[4], N_REP * ROWS * NCH, SPAN, TOPK, 0).reshape((N_REP, ROWS, NCH, TOPK)),
    }


momentum_decay = 0.9
learn_rate = 0.5

def span_basis(length):
    freq = jnp.arange(length, dtype=jnp.float32)[:, None]
    place = jnp.arange(length, dtype=jnp.float32)[None, :]
    scale = jnp.where(freq == 0.0, jnp.sqrt(1.0 / length), jnp.sqrt(2.0 / length))
    return (scale * jnp.cos(jnp.pi * (2.0 * place + 1.0) * freq / (2.0 * length))).astype(jnp.float32)

def reference(tokens, cotangent, params, momentum, indices):
    basis = span_basis(SPAN)
    slots = jnp.arange(SPAN, dtype=jnp.int32)
    high = lax.Precision.HIGHEST
    kept_list = []
    sent_list = []
    for group in range(N_REP):
        gradient = lax.dot_general(cotangent[group], tokens[group], (((0,), (0,)), ((), ())), preferred_element_type=jnp.float32)
        moved = momentum_decay * momentum[group] + gradient
        blocks = moved.reshape(ROWS, NCH, SPAN)
        coeffs = jnp.einsum('rjn,kn->rjk', blocks, basis, precision=high)
        selector = (indices[group][..., None] == slots).astype(jnp.float32)
        chosen = jnp.einsum('rjc,rjtc->rjt', coeffs, selector, precision=high)
        sent = jnp.einsum('rjt,rjtc->rjc', chosen, selector, precision=high)
        back = jnp.einsum('rjk,kn->rjn', sent, basis, precision=high).reshape(ROWS, D)
        kept_list.append(moved - back)
        sent_list.append(sent)
    total = sent_list[0]
    for group in range(1, N_REP):
        total = total + sent_list[group]
    mean_sent = total / N_REP
    update = jnp.einsum('rjk,kn->rjn', mean_sent, basis, precision=high).reshape(ROWS, D)
    return (params - learn_rate * update, jnp.stack(kept_list))
```

```python
import jax, numpy as np
import jax.numpy as jnp
from jax import lax
from jax.sharding import PartitionSpec as P
SPAN = 128
momentum_decay = 0.9
learn_rate = 0.5
def span_basis(length):
    freq = jnp.arange(length, dtype=jnp.float32)[:, None]
    place = jnp.arange(length, dtype=jnp.float32)[None, :]
    scale = jnp.where(freq == 0.0, jnp.sqrt(1.0 / length), jnp.sqrt(2.0 / length))
    return scale * jnp.cos(jnp.pi * (2.0 * place + 1.0) * freq / (2.0 * length))
def reduce_rows(g):
    n = lax.axis_size("fsdp")
    if n % 2 or n > 16:
        return lax.psum_scatter(g, "fsdp", scatter_dimension=0, tiled=True)
    me = lax.axis_index("fsdp")
    rest = n // 2
    width = g.shape[1]
    v = g.reshape(rest, 2, g.shape[0] // n, width)
    mine = lax.dynamic_index_in_dim(v, me % 2, 1, False)
    theirs = lax.dynamic_index_in_dim(v, 1 - me % 2, 1, False)
    part = mine + lax.ppermute(theirs, "fsdp", [(i, i ^ 1) for i in range(n)])
    out = None
    for s in range(rest):
        x = lax.dynamic_index_in_dim(part, (me // 2 + s) % rest, 0, False)
        if s:
            x = lax.ppermute(x, "fsdp", [(i, ((i // 2 + s) % rest) * 2 + i % 2) for i in range(n)])
        out = x if out is None else out + x
    return out


def local(tokens, cotangent, params, momentum, indices):
    tok = tokens[0]; cot = cotangent[0]
    width = tok.shape[1]; nb = width // SPAN
    high = lax.Precision.HIGHEST
    basis = span_basis(SPAN)
    slots = jnp.arange(SPAN, dtype=jnp.int32)
    g = lax.dot_general(cot, tok, (((0,), (0,)), ((), ())), preferred_element_type=jnp.float32)
    grad = reduce_rows(g)
    rows = grad.shape[0]
    moved = momentum_decay * momentum[0] + grad
    coeffs = jnp.einsum("rjn,kn->rjk", moved.reshape(rows, nb, SPAN), basis, precision=high)
    mask = (indices[0][..., None] == slots).any(2)
    sent = jnp.where(mask, coeffs, 0.0)
    back = jnp.einsum("rjk,kn->rjn", sent, basis, precision=high).reshape(rows, width)
    kept = moved - back
    reps = lax.axis_size("rep")
    if reps == 2:
        total = back + lax.ppermute(back, "rep", [(0, 1), (1, 0)])
    else:
        total = lax.psum(back, "rep")
    return params - learn_rate / reps * total, kept[None]
def solution(mesh):
    in_specs = (
        P("rep", ("parts", "fsdp"), None), P("rep", ("parts", "fsdp"), None), P(("parts", "fsdp"), None),
        P("rep", ("parts", "fsdp"), None), P("rep", ("parts", "fsdp"), None, None))
    out_specs = (P(("parts", "fsdp"), None), P("rep", ("parts", "fsdp"), None))
    return jax.shard_map(local, mesh=mesh, in_specs=in_specs, out_specs=out_specs, check_vma=False)
```

```python
import jax
import jax.numpy as jnp
import numpy as np
from jax import lax
from jax.experimental import pallas as pl
from jax.experimental.pallas import tpu as pltpu
from jax.sharding import PartitionSpec as P

SPAN = 128

momentum_decay = 0.9
learn_rate = 0.5


def span_basis(length):
    freq = np.arange(length, dtype=np.float64)[:, None]
    place = np.arange(length, dtype=np.float64)[None, :]
    scale = np.where(freq == 0.0, np.sqrt(1.0 / length), np.sqrt(2.0 / length))
    return scale * np.cos(np.pi * (2.0 * place + 1.0) * freq / (2.0 * length))


def split_factor(matrix):
    high = matrix.astype(jnp.bfloat16)
    low = (matrix - high.astype(np.float64)).astype(jnp.bfloat16)
    return np.block([[high, low], [high, low]])


def split_dot(x, factor):
    high = x.astype(jnp.bfloat16)
    low = (x - high.astype(jnp.float32)).astype(jnp.bfloat16)
    y = jnp.dot(jnp.concatenate([high, low], 1), factor, preferred_element_type=jnp.float32)
    half = y.shape[1] // 2
    return y[:, :half] + y[:, half:]


def select_kernel(count, *refs):
    terms, (momentum, mask, forward, inverse, total, lost) = refs[:count], refs[count:]
    moved = momentum_decay * momentum[...]
    for term in terms:
        moved = moved + term[...]
    coeffs = split_dot(moved, forward[...])
    sent = jnp.where(mask[...] > 0.0, coeffs, 0.0)
    total[...] = moved
    lost[...] = split_dot(sent, inverse[...])


def select(terms, momentum, indices):
    blocks = momentum.size // SPAN
    terms = [t.reshape(blocks, SPAN) for t in terms]
    slots = jnp.arange(SPAN, dtype=jnp.int32)
    mask = jnp.any(indices.reshape(blocks, -1, 1) == slots, 1).astype(jnp.float32)
    basis = span_basis(SPAN)
    shape = jax.ShapeDtypeStruct((blocks, SPAN), jnp.float32)
    vmem = pl.BlockSpec(memory_space=pltpu.VMEM)
    moved, lost = pl.pallas_call(
        lambda *refs: select_kernel(len(terms), *refs),
        out_shape=(shape, shape),
        in_specs=[vmem] * (len(terms) + 4),
        out_specs=(vmem, vmem),
        compiler_params=pltpu.CompilerParams(vmem_limit_bytes=4 << 20),
        name="select",
    )(*terms, momentum.reshape(blocks, SPAN), mask, split_factor(basis.T), split_factor(basis))
    return moved, lost


def staged(n):
    return n in (4, 8, 16)


def send(x, n, reps, offset):
    pairs = [(i * reps + c, (i ^ offset) * reps + (c + 1) % reps) for i in range(n) for c in range(reps)]
    return lax.ppermute(x, ("fsdp", "rep"), pairs)


def near_rows(cot, tok, me, n):
    place = jnp.arange(n, dtype=jnp.int32)
    wanted = (place // (n // 4)) ^ (place % (n // 4) * 4) ^ me
    picked = (wanted[:, None] == place).astype(cot.dtype)
    left = lax.dot_general(picked, cot, (((1,), (1,)), ((), ())), preferred_element_type=jnp.float32)
    left = lax.optimization_barrier(left.astype(cot.dtype).reshape(4, n // 4, -1))
    return lax.dot_general(left, tok, (((2,), (0,)), ((), ())), preferred_element_type=jnp.float32)


def local(tokens, cotangent, params, momentum, indices):
    tok, cot = tokens[0], cotangent[0]
    n, reps = lax.axis_size("fsdp"), lax.axis_size("rep")
    if staged(n) and reps == 2 and params.shape[0] == 1:
        own, *rest = near_rows(cot, tok, lax.axis_index("fsdp"), n)
        arrived = [send(x, n, reps, k) for k, x in enumerate(rest, 1)]
        part = send(own, n, reps, 0)
        for x in arrived:
            part = part + x
        terms = []
        for k in range(n // 4):
            terms.append(send(part[k : k + 1], n, reps, 4 * k))
    else:
        gradient = lax.dot_general(cot, tok, (((0,), (0,)), ((), ())), preferred_element_type=jnp.float32)
        terms = [lax.psum_scatter(gradient, "fsdp", scatter_dimension=0, tiled=True)]
    moved, lost = select(terms, momentum, indices)
    if reps == 2:
        back = lost.reshape(params.shape)
        total = back + send(back, n, reps, 0)
    else:
        total = lax.psum(lost.reshape(params.shape), "rep")
    return params - learn_rate / reps * total, (moved - lost).reshape(momentum.shape)


def solution(mesh):
    in_specs = (
        P("rep", ("parts", "fsdp"), None),
        P("rep", ("parts", "fsdp"), None),
        P(("parts", "fsdp"), None),
        P("rep", ("parts", "fsdp"), None),
        P("rep", ("parts", "fsdp"), None, None),
    )
    out_specs = (P(("parts", "fsdp"), None), P("rep", ("parts", "fsdp"), None))
    return jax.shard_map(local, mesh=mesh, in_specs=in_specs, out_specs=out_specs, check_vma=False)
```

```python
import jax
import jax.numpy as jnp
import numpy as np
from jax import lax
from jax.experimental import pallas as pl
from jax.experimental.pallas import tpu as pltpu
from jax.sharding import PartitionSpec as P

SPAN = 128

momentum_decay = 0.9
learn_rate = 0.5


def span_basis(length):
    freq = np.arange(length, dtype=np.float64)[:, None]
    place = np.arange(length, dtype=np.float64)[None, :]
    scale = np.where(freq == 0.0, np.sqrt(1.0 / length), np.sqrt(2.0 / length))
    return scale * np.cos(np.pi * (2.0 * place + 1.0) * freq / (2.0 * length))


def split_factor(matrix):
    high = matrix.astype(jnp.bfloat16)
    low = (matrix - high.astype(np.float64)).astype(jnp.bfloat16)
    return np.concatenate([high, low], 1)


def split_dot(x, factor):
    high = x.astype(jnp.bfloat16)
    low = (x - high.astype(jnp.float32)).astype(jnp.bfloat16)
    y = jnp.dot(jnp.concatenate([high, low], 0), factor, preferred_element_type=jnp.float32)
    rows, half = x.shape[0], y.shape[1] // 2
    return (y[:rows, :half] + y[rows:, :half]) + (y[:rows, half:] + y[rows:, half:])


def select_kernel(count, *refs):
    terms, (momentum, mask, forward, inverse, total, lost) = refs[:count], refs[count:]
    moved = momentum_decay * momentum[...]
    for term in terms:
        moved = moved + term[...]
    coeffs = split_dot(moved, forward[...])
    sent = jnp.where(mask[...] > 0.0, coeffs, 0.0)
    total[...] = moved
    lost[...] = split_dot(sent, inverse[...])


def select(terms, momentum, indices):
    blocks = momentum.size // SPAN
    terms = [t.reshape(blocks, SPAN) for t in terms]
    slots = jnp.arange(SPAN, dtype=jnp.int32)
    mask = jnp.any(indices.reshape(blocks, -1, 1) == slots, 1).astype(jnp.float32)
    basis = span_basis(SPAN)
    shape = jax.ShapeDtypeStruct((blocks, SPAN), jnp.float32)
    vmem = pl.BlockSpec(memory_space=pltpu.VMEM)
    moved, lost = pl.pallas_call(
        lambda *refs: select_kernel(len(terms), *refs),
        out_shape=(shape, shape),
        in_specs=[vmem] * (len(terms) + 4),
        out_specs=(vmem, vmem),
        compiler_params=pltpu.CompilerParams(vmem_limit_bytes=4 << 20),
        name="select",
    )(*terms, momentum.reshape(blocks, SPAN), mask, split_factor(basis.T), split_factor(basis))
    return moved, lost


def staged(n):
    return n in (4, 8, 16)


def send(x, n, reps, offset):
    pairs = [(i * reps + c, (i ^ offset) * reps + (c + 1) % reps) for i in range(n) for c in range(reps)]
    return lax.ppermute(x, ("fsdp", "rep"), pairs)


def chunk_starts(width):
    blocks = width // SPAN
    return [blocks * f // 40 * SPAN for f in (0, 6, 16, 28, 40)]


def rows_kernel(n, where, cot_hbm, tok, *refs):
    outs, (cot, held, sems) = refs[:-3], refs[-3:]
    width = held.shape[1]
    starts = chunk_starts(width)
    first = pltpu.make_async_copy(cot_hbm, cot, sems.at[len(starts) - 1])
    first.start()
    copies = []
    for c, (a, b) in enumerate(zip(starts, starts[1:])):
        cols = pl.ds(a, b - a)
        copies.append(pltpu.make_async_copy(tok.at[:, cols], held.at[:, cols], sems.at[c]))
        copies[-1].start()
    row = lax.broadcasted_iota(jnp.int32, (n, n), 0)
    col = lax.broadcasted_iota(jnp.int32, (n, n), 1)
    high = n // 4
    picked = ((row // high) ^ (row % high * 4) ^ where[0]) == col
    first.wait()
    left = jnp.dot(picked.astype(cot.dtype), cot[...], preferred_element_type=jnp.float32).astype(cot.dtype)
    for copy, a, b in zip(copies, starts, starts[1:]):
        copy.wait()
        cols = pl.ds(a, b - a)
        y = jnp.dot(left, held[:, cols], preferred_element_type=jnp.float32)
        for k, out in enumerate(outs):
            out[:, cols] = y[high * k : high * (k + 1)]


def near_rows(cot, tok, me, n):
    depth, width = tok.shape
    vmem = pl.BlockSpec(memory_space=pltpu.VMEM)
    hbm = pl.BlockSpec(memory_space=pltpu.HBM)
    tok = pltpu.with_memory_space_constraint(tok, pltpu.HBM)
    cot = pltpu.with_memory_space_constraint(cot.T, pltpu.HBM)
    return pl.pallas_call(
        lambda *refs: rows_kernel(n, *refs),
        out_shape=[jax.ShapeDtypeStruct((n // 4, width), jnp.float32)] * 4,
        in_specs=[pl.BlockSpec(memory_space=pltpu.SMEM), hbm, hbm],
        out_specs=[vmem] * 4,
        scratch_shapes=[
            pltpu.VMEM((n, depth), tok.dtype),
            pltpu.VMEM((depth, width), tok.dtype),
            pltpu.SemaphoreType.DMA((len(chunk_starts(width)),)),
        ],
        compiler_params=pltpu.CompilerParams(vmem_limit_bytes=8 << 20),
        name="near_rows",
    )(me.reshape(1), cot, tok)


def local(tokens, cotangent, params, momentum, indices):
    tok, cot = tokens[0], cotangent[0]
    n, reps = lax.axis_size("fsdp"), lax.axis_size("rep")
    if staged(n) and reps == 2 and params.shape[0] == 1:
        own, *rest = near_rows(cot, tok, lax.axis_index("fsdp"), n)
        arrived = [send(x, n, reps, k) for k, x in enumerate(rest, 1)]
        part = send(own, n, reps, 0)
        for x in arrived:
            part = part + x
        terms = []
        for k in range(n // 4):
            terms.append(send(part[k : k + 1], n, reps, 4 * k))
    else:
        gradient = lax.dot_general(cot, tok, (((0,), (0,)), ((), ())), preferred_element_type=jnp.float32)
        terms = [lax.psum_scatter(gradient, "fsdp", scatter_dimension=0, tiled=True)]
    moved, lost = select(terms, momentum, indices)
    if reps == 2:
        back = lost.reshape(params.shape)
        total = back + send(back, n, reps, 0)
    else:
        total = lax.psum(lost.reshape(params.shape), "rep")
    return params - learn_rate / reps * total, (moved - lost).reshape(momentum.shape)


def solution(mesh):
    in_specs = (
        P("rep", ("parts", "fsdp"), None),
        P("rep", ("parts", "fsdp"), None),
        P(("parts", "fsdp"), None),
        P("rep", ("parts", "fsdp"), None),
        P("rep", ("parts", "fsdp"), None, None),
    )
    out_specs = (P(("parts", "fsdp"), None), P("rep", ("parts", "fsdp"), None))
    return jax.shard_map(local, mesh=mesh, in_specs=in_specs, out_specs=out_specs, check_vma=False)
```

```python
import jax
import jax.numpy as jnp
import numpy as np
from jax import lax
from jax.experimental import pallas as pl
from jax.experimental.pallas import tpu as pltpu
from jax.sharding import PartitionSpec as P

SPAN = 128

momentum_decay = 0.9
learn_rate = 0.5


def span_basis(length):
    freq = np.arange(length, dtype=np.float64)[:, None]
    place = np.arange(length, dtype=np.float64)[None, :]
    scale = np.where(freq == 0.0, np.sqrt(1.0 / length), np.sqrt(2.0 / length))
    return scale * np.cos(np.pi * (2.0 * place + 1.0) * freq / (2.0 * length))


def split_factor(matrix):
    high = matrix.astype(jnp.bfloat16)
    low = (matrix - high.astype(np.float64)).astype(jnp.bfloat16)
    return np.concatenate([high, low], 1)


def split_dot(x, factor):
    high = x.astype(jnp.bfloat16)
    low = (x - high.astype(jnp.float32)).astype(jnp.bfloat16)
    y = jnp.dot(jnp.concatenate([high, low], 0), factor, preferred_element_type=jnp.float32)
    rows, half = x.shape[0], y.shape[1] // 2
    return (y[:rows, :half] + y[rows:, :half]) + (y[:rows, half:] + y[rows:, half:])


def select_kernel(count, *refs):
    terms, (momentum, mask, forward, inverse, total, lost) = refs[:count], refs[count:]
    moved = momentum_decay * momentum[...]
    for term in terms:
        moved = moved + term[...]
    coeffs = split_dot(moved, forward[...])
    sent = jnp.where(mask[...] > 0.0, coeffs, 0.0)
    total[...] = moved
    lost[...] = split_dot(sent, inverse[...])


def select(terms, momentum, indices):
    blocks = momentum.size // SPAN
    terms = [t.reshape(blocks, SPAN) for t in terms]
    slots = jnp.arange(SPAN, dtype=jnp.int32)
    mask = jnp.any(indices.reshape(blocks, -1, 1) == slots, 1).astype(jnp.float32)
    basis = span_basis(SPAN)
    shape = jax.ShapeDtypeStruct((blocks, SPAN), jnp.float32)
    vmem = pl.BlockSpec(memory_space=pltpu.VMEM)
    moved, lost = pl.pallas_call(
        lambda *refs: select_kernel(len(terms), *refs),
        out_shape=(shape, shape),
        in_specs=[vmem] * (len(terms) + 4),
        out_specs=(vmem, vmem),
        compiler_params=pltpu.CompilerParams(vmem_limit_bytes=4 << 20),
        name="select",
    )(*terms, momentum.reshape(blocks, SPAN), mask, split_factor(basis.T), split_factor(basis))
    return moved, lost


def staged(n):
    return n in (4, 8, 16)


def turned(i, k):
    return 3 - k if k in (1, 2) and (i ^ (i >> 1)) & 1 else k


def send(x, n, reps, offset):
    to = [i ^ turned(i, offset) for i in range(n)]
    pairs = [(i * reps + c, to[i] * reps + (c + 1) % reps) for i in range(n) for c in range(reps)]
    return lax.ppermute(x, ("fsdp", "rep"), pairs)


def chunk_starts(width):
    blocks = width // SPAN
    return [blocks * f // 40 * SPAN for f in (0, 6, 16, 28, 40)]


def rows_kernel(n, where, cot_hbm, tok, *refs):
    outs, (cot, held, sems) = refs[:-3], refs[-3:]
    width = held.shape[1]
    starts = chunk_starts(width)
    first = pltpu.make_async_copy(cot_hbm, cot, sems.at[len(starts) - 1])
    first.start()
    copies = []
    for c, (a, b) in enumerate(zip(starts, starts[1:])):
        cols = pl.ds(a, b - a)
        copies.append(pltpu.make_async_copy(tok.at[:, cols], held.at[:, cols], sems.at[c]))
        copies[-1].start()
    row = lax.broadcasted_iota(jnp.int32, (n, n), 0)
    col = lax.broadcasted_iota(jnp.int32, (n, n), 1)
    high = n // 4
    piece, me = row // high, where[0]
    swapped = jnp.where((piece == 1) | (piece == 2), 3 - piece, piece)
    odd = (me ^ (me // 2)) % 2
    piece = jnp.where(odd == 1, swapped, piece)
    picked = (piece ^ (row % high * 4) ^ me) == col
    first.wait()
    left = jnp.dot(picked.astype(cot.dtype), cot[...], preferred_element_type=jnp.float32).astype(cot.dtype)
    for copy, a, b in zip(copies, starts, starts[1:]):
        copy.wait()
        cols = pl.ds(a, b - a)
        y = jnp.dot(left, held[:, cols], preferred_element_type=jnp.float32)
        for k, out in enumerate(outs):
            out[:, cols] = y[high * k : high * (k + 1)]


def near_rows(cot, tok, me, n):
    depth, width = tok.shape
    vmem = pl.BlockSpec(memory_space=pltpu.VMEM)
    hbm = pl.BlockSpec(memory_space=pltpu.HBM)
    tok = pltpu.with_memory_space_constraint(tok, pltpu.HBM)
    cot = pltpu.with_memory_space_constraint(cot.T, pltpu.HBM)
    return pl.pallas_call(
        lambda *refs: rows_kernel(n, *refs),
        out_shape=[jax.ShapeDtypeStruct((n // 4, width), jnp.float32)] * 4,
        in_specs=[pl.BlockSpec(memory_space=pltpu.SMEM), hbm, hbm],
        out_specs=[vmem] * 4,
        scratch_shapes=[
            pltpu.VMEM((n, depth), tok.dtype),
            pltpu.VMEM((depth, width), tok.dtype),
            pltpu.SemaphoreType.DMA((len(chunk_starts(width)),)),
        ],
        compiler_params=pltpu.CompilerParams(vmem_limit_bytes=8 << 20),
        name="near_rows",
    )(me.reshape(1), cot, tok)


def local(tokens, cotangent, params, momentum, indices):
    tok, cot = tokens[0], cotangent[0]
    n, reps = lax.axis_size("fsdp"), lax.axis_size("rep")
    if staged(n) and reps == 2 and params.shape[0] == 1:
        own, *rest = near_rows(cot, tok, lax.axis_index("fsdp"), n)
        arrived = [send(x, n, reps, k) for k, x in enumerate(rest, 1)]
        part = send(own, n, reps, 0)
        for x in arrived:
            part = part + x
        terms = []
        for k in range(n // 4):
            terms.append(send(part[k : k + 1], n, reps, 4 * k))
    else:
        gradient = lax.dot_general(cot, tok, (((0,), (0,)), ((), ())), preferred_element_type=jnp.float32)
        terms = [lax.psum_scatter(gradient, "fsdp", scatter_dimension=0, tiled=True)]
    moved, lost = select(terms, momentum, indices)
    if reps == 2:
        back = lost.reshape(params.shape)
        total = back + send(back, n, reps, 0)
    else:
        total = lax.psum(lost.reshape(params.shape), "rep")
    return params - learn_rate / reps * total, (moved - lost).reshape(momentum.shape)


def solution(mesh):
    in_specs = (
        P("rep", ("parts", "fsdp"), None),
        P("rep", ("parts", "fsdp"), None),
        P(("parts", "fsdp"), None),
        P("rep", ("parts", "fsdp"), None),
        P("rep", ("parts", "fsdp"), None, None),
    )
    out_specs = (P(("parts", "fsdp"), None), P("rep", ("parts", "fsdp"), None))
    return jax.shard_map(local, mesh=mesh, in_specs=in_specs, out_specs=out_specs, check_vma=False)
```
